256 devices in a mesh: blk: 64 (over x, y_hi, z), con: 4 (over y_lo, core).
Axes of the slice: x: 4, y: 4 (y_hi: 2, y_lo: 2; y = y_hi * 2 + y_lo), z: 8, core: 2. Of those that a mesh axis runs over, the one named last changes fastest.
Arguments:
- patch_rows: bfloat16 [4, 12288, 16, 1024], P('con', 'blk'), may hold values from -6 to 6
- subject_ids: int32 [12288], replicated, may hold values from 0 to 3071
- logit_scale: float32 [2], replicated, may hold values from 5 to 20
- logit_bias: float32 [2], replicated, may hold values from -6 to -2
Outputs:
- grad_emb: float32 [4, 12288, 1024], P('con', 'blk')
The draws below stay inside these ranges and needn't reach their ends.
All inputs are finite; a program needn't handle non-finite values.
Results may differ from the reference program's by a relative error of at most 0.0037.
Values may be sent and summed in bfloat16 or wider, within the bound.
No kernel may reach another device: no remote copies, remote signals or barrier semaphores. Data moves between devices by JAX's collectives and lax.ppermute only.
A program may use at most 128 MiB of HBM per device.

```python
import math
import jax
import jax.numpy as jnp
from jax import lax

D = 1024
PATCHES = 16
B = 12288
CONTRASTS = 4
PAIRS = 2


def place_ends(result, rng, least, largest):
    index_at = [jax.random.randint(jax.random.fold_in(rng, axis), (), 0, length) for axis, length in enumerate(result.shape)]
    main_axis = result.shape.index(max(result.shape))
    next_to = index_at[:main_axis] + [(index_at[main_axis] + 1) % result.shape[main_axis]] + index_at[main_axis + 1:]
    return result.at[tuple(index_at)].set(least).at[tuple(next_to)].set(largest)


def level_of(key, shape, split, least, top_value):
    level = 1.0
    for position, blocks in split:
        draws = jax.random.uniform(jax.random.fold_in(jax.random.fold_in(key, 6), position), (blocks,), jnp.float32, least / len(split), top_value / len(split))
        level = level * jnp.repeat(jnp.exp(draws), shape[position] // blocks).reshape((-1,) + (1,) * (len(shape) - 1 - position))
    return level


def normal_values(stream_key, dims, deviation, bound, cuts=(), kind=jnp.bfloat16):
    entries = deviation * jax.random.normal(stream_key, dims, jnp.float32)
    if cuts:
        entries = entries * level_of(stream_key, dims, cuts, -0.22, 0.18)
    return jnp.clip(entries, -bound, bound).astype(kind)


def setup_inputs(seed: int = 0) -> dict:
    keys = jax.random.split(jax.random.key(seed), 5)
    return {
        "patch_rows": normal_values(keys[0], (CONTRASTS, B, PATCHES, D), 1.0, 6.0, ((0, 4), (1, 64))),
        "subject_ids": place_ends(jax.random.randint(keys[1], (B,), 0, B // 4), jax.random.fold_in(keys[1], 1), 0, (B // 4) - 1).astype(jnp.int32),
        "logit_scale": jnp.clip(jnp.exp(jax.random.uniform(keys[2], (PAIRS,), jnp.float32, math.log(5.0), math.log(20.0))), 5.0, 20.0),
        "logit_bias": jnp.clip(jax.random.uniform(keys[3], (PAIRS,), jnp.float32, -6.0, -2.0), -6.0, -2.0),
    }


def pair_grads(first_emb, second_emb, subject_ids, scale_value, bias_value):
    block = math.gcd(B, 512)

    def scan_rows(grad_second, block_index):
        first_row = (block_index * block).astype(jnp.int32)
        first_block = lax.dynamic_slice_in_dim(first_emb, first_row, block, 0)
        block_ids = lax.dynamic_slice_in_dim(subject_ids, first_row, block, 0)
        logits = scale_value * lax.dot_general(first_block, second_emb, (((1,), (1,)), ((), ())), preferred_element_type=jnp.float32) + bias_value
        label_sign = jnp.where(block_ids[:, None] == subject_ids[None, :], 1.0, -1.0).astype(jnp.float32)
        coeff = (scale_value * (jax.nn.sigmoid(label_sign * logits) - 1.0) * label_sign).astype(jnp.bfloat16)
        grad_block = jnp.dot(coeff, second_emb, preferred_element_type=jnp.float32)
        grad_second = grad_second + lax.dot_general(coeff, first_block, (((0,), (0,)), ((), ())), preferred_element_type=jnp.float32)
        return (grad_second, grad_block)
    grad_second, grad_blocks = lax.scan(scan_rows, jnp.zeros((B, D), jnp.float32), jnp.arange(B // block).astype(jnp.int32))
    return (grad_blocks.reshape(B, D), grad_second)

def reference(patch_rows, subject_ids, logit_scale, logit_bias):
    pooled = lax.optimization_barrier(jnp.sum(patch_rows, axis=2, dtype=jnp.float32)) / PATCHES
    row_norms = jnp.sqrt(lax.optimization_barrier(jnp.sum(pooled * pooled, axis=2, keepdims=True)) + 1e-06)
    emb = (pooled / row_norms).astype(jnp.bfloat16)
    results = []
    for pair_index in range(PAIRS):
        grad_first, grad_second = pair_grads(emb[2 * pair_index], emb[2 * pair_index + 1], subject_ids, logit_scale[pair_index], logit_bias[pair_index])
        results.append(grad_first)
        results.append(grad_second)
    return jnp.stack(results, axis=0)
```

```python
import jax
import jax.numpy as jnp
from jax import lax
from jax.sharding import PartitionSpec as P

AXES = ("blk", "con")
NX, NYH, NZ, NYL, NC = 4, 2, 8, 2, 2


def flat(x, yh, z, yl, c):
    return (((x % NX) * NYH + yh % NYH) * NZ + z % NZ) * 4 + yl * NC + c


def perm(first, second):
    pairs = []
    for x in range(NX):
        for yh in range(NYH):
            for z in range(NZ):
                for yl in range(NYL):
                    for c, move in ((0, first), (1, second)):
                        if move is not None:
                            pairs.append((flat(x, yh, z, yl, c), flat(x + move[0], yh + move[1], z + move[2], yl, c)))
    return pairs


def partner(v):
    n = NX * NYH * NZ * 4
    return lax.ppermute(v, AXES, [(i, i ^ 1) for i in range(n)])


ZP, ZM, XP, XM, YX = (0, 0, 1), (0, 0, -1), (1, 0, 0), (-1, 0, 0), (0, 1, 0)


def send(v, first, second):
    return lax.ppermute(v, AXES, perm(first, second))


def on_device(patch_rows, subject_ids, logit_scale, logit_bias):
    n, patches, width = patch_rows.shape[1:]
    pooled = jnp.sum(patch_rows[0], axis=1, dtype=jnp.float32) / patches
    norms = jnp.sqrt(jnp.sum(pooled * pooled, axis=1, keepdims=True) + 1e-06)
    own = (pooled / norms).astype(jnp.bfloat16)

    con = lax.axis_index("con")
    blk = lax.axis_index("blk")
    core = con % 2
    is0 = core == 0
    scale = logit_scale[con // 2]
    bias = logit_bias[con // 2]
    x, yh, z = blk // 16, (blk // 8) % 2, blk % 8

    half = n // 2
    p1 = send(own, ZP, XP)
    m1 = send(own, ZM, XM)
    yy = send(own, None, YX)
    p2 = send(jnp.where(is0, p1, yy), ZP, XP)
    m2 = send(jnp.where(is0, m1, yy), ZM, XM)
    p3 = send(jnp.where(is0, p2, p1), ZP, XP)
    m3 = send(m2, ZM, XM)
    s4a = send(p3[:half], ZP, None)
    s4b = send(m3[half:], ZM, None)
    s7 = jnp.where(is0, jnp.concatenate([s4a, s4b]), yy)
    slots = [own, p1, m1, p2, m2, p3, m3, s7]
    mine = jnp.concatenate(slots)
    other = jnp.concatenate([partner(v) for v in slots])

    z_off = (0, -1, 1, -2, 2, -3, 3, 4)
    x_off = (0, -1, 1, -1, 1, -2, 2, 0)
    y_off = (0, 0, 0, 1, 1, 0, 1, 1)

    def ids(first):
        parts = []
        for zo, xo, yo in zip(z_off, x_off, y_off):
            on_z = (x * NYH + yh) * NZ + (z + zo) % NZ
            on_xy = (((x + xo) % NX) * NYH + (yh + yo) % NYH) * NZ + z
            parts.append(lax.dynamic_slice_in_dim(subject_ids, jnp.where(first, on_z, on_xy) * n, n, 0))
        return jnp.concatenate(parts)

    row_ids, col_ids = ids(is0), ids(core == 1)
    logits = scale * lax.dot_general(mine, other, (((1,), (1,)), ((), ())), preferred_element_type=jnp.float32) + bias
    sign = jnp.where(row_ids[:, None] == col_ids[None, :], 1.0, -1.0).astype(jnp.float32)
    coeff = (scale * (jax.nn.sigmoid(sign * logits) - 1.0) * sign).astype(jnp.bfloat16)
    g = jnp.dot(coeff, other, preferred_element_type=jnp.float32)
    g0, gp1, gm1, gp2, gm2, gp3, gm3, g7 = [g[i * n:(i + 1) * n] for i in range(8)]

    bf = lambda v: v.astype(jnp.bfloat16)
    f = lambda v: v.astype(jnp.float32)
    on0 = lambda v: jnp.where(is0, f(v), 0.0)
    on1 = lambda v: jnp.where(is0, 0.0, f(v))
    r4a = send(bf(g7[:half]), ZM, None)
    r4b = send(bf(g7[half:]), ZP, None)
    gp3 = jnp.concatenate([gp3[:half] + f(r4a), gp3[half:]])
    gm3 = jnp.concatenate([gm3[:half], gm3[half:] + f(r4b)])
    rp3 = send(bf(gp3), ZM, XM)
    rm3 = send(bf(gm3), ZP, XP)
    gp2 = gp2 + on0(rp3)
    gm2 = gm2 + f(rm3)
    rp2 = send(bf(gp2), ZM, XM)
    rm2 = send(bf(gm2), ZP, XP)
    gp1 = gp1 + on1(rp3) + on0(rp2)
    gm1 = gm1 + on0(rm2)
    g7 = g7 + on1(rp2) + on1(rm2)
    rp1 = send(bf(gp1), ZM, XM)
    rm1 = send(bf(gm1), ZP, XP)
    ry = send(bf(g7), None, YX)
    out = g0 + f(rp1) + f(rm1) + f(ry)
    return out.reshape(1, n, width)


def solution(mesh):
    in_specs = (P("con", "blk", None, None), P(), P(), P())
    return jax.shard_map(on_device, mesh=mesh, in_specs=in_specs, out_specs=P("con", "blk", None), check_vma=False)
```

```python
import functools
import jax
import jax.numpy as jnp
from jax import lax
from jax.experimental import pallas as pl
from jax.experimental.pallas import tpu as pltpu
from jax.sharding import PartitionSpec as P

AXES = ("blk", "con")
NX, NYH, NZ, NYL = 4, 2, 8, 2
VMEM_LIMIT = 14 * 1024 * 1024
NT = (((1,), (1,)), ((), ()))


def flat(x, yh, z, yl, c):
    return (((x % NX) * NYH + yh % NYH) * NZ + z % NZ) * 4 + yl * 2 + c


def send(v, ways):
    pairs = []
    for x in range(NX):
        for yh in range(NYH):
            for z in range(NZ):
                for yl in range(NYL):
                    for c, way in enumerate(ways):
                        dx, dy, dz = way(z) if callable(way) else way
                        pairs.append((flat(x, yh, z, yl, c), flat(x + dx, yh + dy, z + dz, yl, c)))
    return lax.ppermute(v, AXES, pairs)


def partner(v):
    return lax.ppermute(v, AXES, [(i, i ^ 1) for i in range(NX * NYH * NZ * 4)])


POOL_STEP = 32


def pool_kernel(x_ref, o_ref, buf, sems):
    n, patches, width = buf.shape
    copies = [
        pltpu.make_async_copy(x_ref.at[pl.ds(i, POOL_STEP)], buf.at[pl.ds(i, POOL_STEP)], sems.at[i // POOL_STEP])
        for i in range(0, n, POOL_STEP)
    ]
    for copy in copies:
        copy.start()
    row = lax.broadcasted_iota(jnp.int32, (POOL_STEP, POOL_STEP * patches), 0) * patches
    col = lax.broadcasted_iota(jnp.int32, (POOL_STEP, POOL_STEP * patches), 1)
    pick = jnp.where((col >= row) & (col < row + patches), 1.0, 0.0).astype(jnp.bfloat16)
    for i, copy in zip(range(0, n, POOL_STEP), copies):
        copy.wait()
        flat_rows = buf[i:i + POOL_STEP].reshape(POOL_STEP * patches, width)
        pooled = jnp.dot(pick, flat_rows, preferred_element_type=jnp.float32) * (1.0 / patches)
        square = jnp.sum(pooled * pooled, axis=1, keepdims=True)
        o_ref[i:i + POOL_STEP, :] = (pooled * (1.0 / jnp.sqrt(square + 1e-06))).astype(o_ref.dtype)


def pool(rows):
    n, _, width = rows.shape
    return pl.pallas_call(
        pool_kernel,
        in_specs=[pl.BlockSpec(memory_space=pltpu.HBM)],
        out_specs=pl.BlockSpec(memory_space=pltpu.VMEM),
        out_shape=jax.ShapeDtypeStruct((n, width), jnp.bfloat16),
        scratch_shapes=[pltpu.VMEM(rows.shape, rows.dtype), pltpu.SemaphoreType.DMA((n // POOL_STEP,))],
        compiler_params=pltpu.CompilerParams(vmem_limit_bytes=60 * 1024 * 1024),
        cost_estimate=pl.CostEstimate(flops=2 * rows.size, bytes_accessed=2 * rows.size, transcendentals=0),
        name="pool",
    )(rows)


def grad_kernel(slots, first_col, groups, has_sum, par_ref, row_ref, col_ref, *refs):
    count = len(slots)
    s_refs, t_refs = refs[:count], refs[count:count + 4 * groups]
    sum_refs, o_refs = (refs[-2 * count:-count], refs[-count:]) if has_sum else (None, refs[-count:])
    pair = lax.axis_index("con") // 2
    scale, bias = par_ref[pl.ds(pair, 1), :], par_ref[pl.ds(pair + 2, 1), :]
    n = s_refs[0].shape[0]
    rows = jnp.concatenate([s[...] for s in s_refs], axis=0)
    row_ids = jnp.concatenate([row_ref[n * k:n * (k + 1), :] for k in slots], axis=0)
    total = jnp.concatenate([v[...] for v in sum_refs], axis=0) if has_sum else None
    for g in range(groups):
        cols = jnp.concatenate([t[...] for t in t_refs[4 * g:4 * g + 4]], axis=0)
        k = cols.shape[0]
        start = first_col * n + g * k
        dots = lax.dot_general(rows, cols, NT, preferred_element_type=jnp.float32)
        same = jnp.concatenate([row_ids] * (k // 128), axis=1) == col_ref[:, start:start + k]
        coeff = scale * jnp.tanh(scale * dots + bias) - jnp.where(same, scale, -scale)
        part = jnp.dot(coeff.astype(jnp.bfloat16), cols, preferred_element_type=jnp.float32)
        total = part if total is None else total + part
    for i, o_ref in enumerate(o_refs):
        o_ref[...] = total[n * i:n * (i + 1)].astype(o_ref.dtype)


def grads(state, slots, first_col, groups, sums, dtype):
    par, row_ids, col_ids, rows, cols = state
    n, width = rows[0].shape
    count = len(slots)
    vmem = pl.BlockSpec(memory_space=pltpu.VMEM)
    operands = [rows[k] for k in slots] + cols[first_col:first_col + 4 * groups] + list(sums or [])
    return pl.pallas_call(
        functools.partial(grad_kernel, slots, first_col, groups, sums is not None),
        in_specs=[vmem] * (3 + len(operands)),
        out_specs=[vmem] * count,
        out_shape=[jax.ShapeDtypeStruct((n, width), dtype)] * count,
        compiler_params=pltpu.CompilerParams(vmem_limit_bytes=VMEM_LIMIT),
        cost_estimate=pl.CostEstimate(flops=16 * groups * count * n * n * width, bytes_accessed=4 * n * width * 2, transcendentals=4 * groups * count * n * n),
    )(par, row_ids, col_ids, *operands)


MOVES = {
    1: ((0, 0, 2), (0, 1, 0)), 2: ((0, 0, -2), (2, 0, 0)), 3: ((0, 0, 1), (1, 0, 0)), 4: ((0, 0, -1), (-1, 0, 0)),
    5: ((0, 0, 1), (1, 0, 0)), 6: ((0, 0, -1), (0, 1, 0)), 7: (lambda z: (0, 0, -2 if z % 2 else 2), (-1, 0, 0)),
}
BACK = {
    k: tuple(((lambda z, way=way: tuple(-d for d in way(z))) if callable(way) else tuple(-d for d in way)) for way in ways)
    for k, ways in MOVES.items()
}
Z_OFF = (0, -2, 2, -1, 1, -3, 3, -4)
X_OFF = (0, 0, 2, -1, 1, -1, 2, 1)
Y_OFF = (0, 1, 0, 0, 0, 1, 1, 1)


def on_device(patch_rows, subject_ids, logit_scale, logit_bias):
    n, _, width = patch_rows.shape[1:]
    f32, bf16 = jnp.float32, jnp.bfloat16
    own = pool(patch_rows[0])

    blk = lax.axis_index("blk")
    first = lax.axis_index("con") % 2 == 0
    x, yh, z = blk // 16, (blk // 8) % 2, blk % 8

    def ids(on_first):
        parts = []
        for zo, xo, yo in zip(Z_OFF, X_OFF, Y_OFF):
            on_z = (x * NYH + yh) * NZ + (z + zo) % NZ
            on_xy = (((x + xo) % NX) * NYH + (yh + yo) % NYH) * NZ + z
            parts.append(lax.dynamic_slice_in_dim(subject_ids, jnp.where(on_first, on_z, on_xy) * n, n, 0))
        return jnp.concatenate(parts)

    par = jnp.broadcast_to(jnp.concatenate([logit_scale, logit_bias])[:, None] * 0.5, (4, 4 * n))
    row_ids = jnp.broadcast_to(ids(first)[:, None], (8 * n, 128))
    col_ids = ids(jnp.logical_not(first))[None, :]

    rows = [own] + [None] * 7
    rows[1] = send(own, MOVES[1])
    rows[2] = send(own, MOVES[2])
    later, par, row_ids, col_ids = lax.optimization_barrier((own, par, row_ids, col_ids))
    rows[3] = send(later, MOVES[3])
    rows[4] = send(later, MOVES[4])
    rows[5] = send(rows[1], MOVES[5])
    turn = jnp.logical_and(first, z % 2 == 1)
    rows[7] = send(jnp.where(turn, rows[2], rows[1]), MOVES[7])
    rows[6] = send(rows[2], MOVES[6])
    cols = [partner(v) for v in rows[:5]]
    state = (par, row_ids, col_ids, rows, cols)
    h0, h3, h4 = grads(state, (0, 3, 4), 0, 1, None, f32)
    h1, h2 = grads(state, (1, 2), 0, 1, None, f32)
    rows[5], rows[6], rows[7], h0, h1, h2, h3, h4 = lax.optimization_barrier((rows[5], rows[6], rows[7], h0, h1, h2, h3, h4))
    cols += [partner(rows[k]) for k in (5, 6, 7)]
    h7, h5 = grads(state, (7, 5), 0, 1, None, f32)
    g7, g5 = grads(state, (7, 5), 4, 1, (h7, h5), bf16)
    rows[6], r7, r5 = lax.optimization_barrier((rows[6], g7, g5))
    r7, r5 = send(r7, BACK[7]), send(r5, BACK[5])
    (g6,) = grads(state, (6,), 0, 2, None, bf16)
    r6 = send(g6, BACK[6])
    g1, g2 = grads(state, (1, 2), 4, 1, (h1, h2), f32)
    g3, g4 = grads(state, (3, 4), 4, 1, (h3, h4), bf16)
    r3 = send(g3, BACK[3])
    r4 = send(g4, BACK[4])
    r7 = r7.astype(f32)
    r1 = send((g1 + jnp.where(turn, 0.0, r7) + r5.astype(f32)).astype(bf16), BACK[1])
    r2 = send((g2 + jnp.where(turn, r7, 0.0) + r6.astype(f32)).astype(bf16), BACK[2])
    (g0,) = grads(state, (0,), 4, 1, (h0,), f32)
    out = g0 + r3.astype(f32) + r4.astype(f32) + r1.astype(f32) + r2.astype(f32)
    return out.reshape(1, n, width)


def solution(mesh):
    in_specs = (P("con", "blk", None, None), P(), P(), P())

    return jax.shard_map(on_device, mesh=mesh, in_specs=in_specs, out_specs=P("con", "blk", None), check_vma=False)
```

```python
import functools
import jax
import jax.numpy as jnp
from jax import lax
from jax.experimental import pallas as pl
from jax.experimental.pallas import tpu as pltpu
from jax.sharding import PartitionSpec as P

AXES = ("blk", "con")
NX, NYH, NZ, NYL = 4, 2, 8, 2
VMEM_LIMIT = 14 * 1024 * 1024
NT = (((1,), (1,)), ((), ()))


def flat(x, yh, z, yl, c):
    return (((x % NX) * NYH + yh % NYH) * NZ + z % NZ) * 4 + yl * 2 + c


def send(v, ways):
    pairs = []
    for x in range(NX):
        for yh in range(NYH):
            for z in range(NZ):
                for yl in range(NYL):
                    for c, way in enumerate(ways):
                        dx, dy, dz = way(z) if callable(way) else way
                        pairs.append((flat(x, yh, z, yl, c), flat(x + dx, yh + dy, z + dz, yl, c)))
    return lax.ppermute(v, AXES, pairs)


def partner(v):
    return lax.ppermute(v, AXES, [(i, i ^ 1) for i in range(NX * NYH * NZ * 4)])


POOL_STEP = 48
PICK = 16


def pool_kernel(x_ref, o_ref, buf, sems):
    n, patches, width = buf.shape
    copies = [
        pltpu.make_async_copy(x_ref.at[pl.ds(i, POOL_STEP)], buf.at[pl.ds(i, POOL_STEP)], sems.at[i // POOL_STEP])
        for i in range(0, n, POOL_STEP)
    ]
    for copy in copies:
        copy.start()
    row = lax.broadcasted_iota(jnp.int32, (PICK, PICK * patches), 0) * patches
    col = lax.broadcasted_iota(jnp.int32, (PICK, PICK * patches), 1)
    pick = jnp.where((col >= row) & (col < row + patches), 1.0, 0.0).astype(jnp.bfloat16)
    for i in range(0, n, PICK):
        if i % POOL_STEP == 0:
            copies[i // POOL_STEP].wait()
        pooled = jnp.dot(pick, buf[i:i + PICK].reshape(PICK * patches, width), preferred_element_type=jnp.float32)
        pooled = pooled * (1.0 / patches)
        square = jnp.sum(pooled * pooled, axis=1, keepdims=True)
        o_ref[i:i + PICK, :] = (pooled * (1.0 / jnp.sqrt(square + 1e-06))).astype(o_ref.dtype)


def pool(rows):
    n, _, width = rows.shape
    return pl.pallas_call(
        pool_kernel,
        in_specs=[pl.BlockSpec(memory_space=pltpu.HBM)],
        out_specs=pl.BlockSpec(memory_space=pltpu.VMEM),
        out_shape=jax.ShapeDtypeStruct((n, width), jnp.bfloat16),
        scratch_shapes=[pltpu.VMEM(rows.shape, rows.dtype), pltpu.SemaphoreType.DMA((n // POOL_STEP,))],
        compiler_params=pltpu.CompilerParams(vmem_limit_bytes=60 * 1024 * 1024),
        cost_estimate=pl.CostEstimate(flops=2 * rows.size, bytes_accessed=2 * rows.size, transcendentals=0),
        name="pool",
    )(rows)


def grad_kernel(slots, first_col, groups, has_sum, par_ref, row_ref, col_ref, *refs):
    count = len(slots)
    s_refs, t_refs = refs[:count], refs[count:count + 4 * groups]
    sum_refs, o_refs = (refs[-2 * count:-count], refs[-count:]) if has_sum else (None, refs[-count:])
    pair = lax.axis_index("con") // 2
    scale, bias = par_ref[pl.ds(pair, 1), :], par_ref[pl.ds(pair + 2, 1), :]
    n = s_refs[0].shape[0]
    rows = jnp.concatenate([s[...] for s in s_refs], axis=0)
    row_ids = jnp.concatenate([row_ref[n * k:n * (k + 1), :] for k in slots], axis=0)
    total = jnp.concatenate([v[...] for v in sum_refs], axis=0) if has_sum else None
    for g in range(groups):
        cols = jnp.concatenate([t[...] for t in t_refs[4 * g:4 * g + 4]], axis=0)
        k = cols.shape[0]
        start = first_col * n + g * k
        dots = lax.dot_general(rows, cols, NT, preferred_element_type=jnp.float32)
        same = jnp.concatenate([row_ids] * (k // 128), axis=1) == col_ref[:, start:start + k]
        coeff = scale * jnp.tanh(scale * dots + bias) - jnp.where(same, scale, -scale)
        part = jnp.dot(coeff.astype(jnp.bfloat16), cols, preferred_element_type=jnp.float32)
        total = part if total is None else total + part
    for i, o_ref in enumerate(o_refs):
        o_ref[...] = total[n * i:n * (i + 1)].astype(o_ref.dtype)


def grads(state, slots, first_col, groups, sums, dtypes):
    par, row_ids, col_ids, rows, cols = state
    n, width = rows[0].shape
    count = len(slots)
    vmem = pl.BlockSpec(memory_space=pltpu.VMEM)
    operands = [rows[k] for k in slots] + cols[first_col:first_col + 4 * groups] + list(sums or [])
    return pl.pallas_call(
        functools.partial(grad_kernel, slots, first_col, groups, sums is not None),
        in_specs=[vmem] * (3 + len(operands)),
        out_specs=[vmem] * count,
        out_shape=[jax.ShapeDtypeStruct((n, width), dtype) for dtype in dtypes],
        compiler_params=pltpu.CompilerParams(vmem_limit_bytes=VMEM_LIMIT),
        cost_estimate=pl.CostEstimate(flops=16 * groups * count * n * n * width, bytes_accessed=4 * n * width * 2, transcendentals=4 * groups * count * n * n),
    )(par, row_ids, col_ids, *operands)


MOVES = {
    1: ((0, 0, 2), (0, 1, 0)), 2: ((0, 0, -2), (2, 0, 0)), 3: ((0, 0, 1), (1, 0, 0)), 4: ((0, 0, -1), (-1, 0, 0)),
    5: ((0, 0, 1), (1, 0, 0)), 6: ((0, 0, -1), (0, 1, 0)), 7: (lambda z: (0, 0, -2 if z % 2 else 2), (-1, 0, 0)),
}
BACK = {
    k: tuple(((lambda z, way=way: tuple(-d for d in way(z))) if callable(way) else tuple(-d for d in way)) for way in ways)
    for k, ways in MOVES.items()
}
Z_OFF = (0, -2, 2, -1, 1, -3, 3, -4)
X_OFF = (0, 0, 2, -1, 1, -1, 2, 1)
Y_OFF = (0, 1, 0, 0, 0, 1, 1, 1)


def on_device(patch_rows, subject_ids, logit_scale, logit_bias):
    n, _, width = patch_rows.shape[1:]
    f32, bf16 = jnp.float32, jnp.bfloat16
    own = pool(patch_rows[0])

    blk = lax.axis_index("blk")
    first = lax.axis_index("con") % 2 == 0
    x, yh, z = blk // 16, (blk // 8) % 2, blk % 8

    def ids(on_first):
        parts = []
        for zo, xo, yo in zip(Z_OFF, X_OFF, Y_OFF):
            on_z = (x * NYH + yh) * NZ + (z + zo) % NZ
            on_xy = (((x + xo) % NX) * NYH + (yh + yo) % NYH) * NZ + z
            parts.append(lax.dynamic_slice_in_dim(subject_ids, jnp.where(on_first, on_z, on_xy) * n, n, 0))
        return jnp.concatenate(parts)

    par = jnp.broadcast_to(jnp.concatenate([logit_scale, logit_bias])[:, None] * 0.5, (4, 4 * n))
    row_ids = jnp.broadcast_to(ids(first)[:, None], (8 * n, 128))
    col_ids = ids(jnp.logical_not(first))[None, :]

    rows = [own] + [None] * 7
    rows[1] = send(own, MOVES[1])
    rows[2] = send(own, MOVES[2])
    later, par, row_ids, col_ids = lax.optimization_barrier((own, par, row_ids, col_ids))
    rows[3] = send(later, MOVES[3])
    rows[4] = send(later, MOVES[4])
    rows[5] = send(rows[1], MOVES[5])
    turn = jnp.logical_and(first, z % 2 == 1)
    rows[7] = send(jnp.where(turn, rows[2], rows[1]), MOVES[7])
    rows[6] = send(rows[2], MOVES[6])
    cols = [partner(v) for v in rows[:5]]
    state = (par, row_ids, col_ids, rows, cols)
    h0, h3, h4 = grads(state, (0, 3, 4), 0, 1, None, (f32,) * 3)
    h1, h2 = grads(state, (1, 2), 0, 1, None, (f32,) * 2)
    rows[5], rows[6], rows[7], h0, h1, h2, h3, h4 = lax.optimization_barrier((rows[5], rows[6], rows[7], h0, h1, h2, h3, h4))
    cols += [partner(rows[k]) for k in (5, 6, 7)]
    h7, h5, h6 = grads(state, (7, 5, 6), 0, 1, None, (f32,) * 3)
    g7, g5, g6 = grads(state, (7, 5, 6), 4, 1, (h7, h5, h6), (bf16,) * 3)
    r7 = send(g7, BACK[7])
    r5 = send(g5, BACK[5])
    r6 = send(g6, BACK[6])
    rows[1], g6 = lax.optimization_barrier((rows[1], g6))
    g1, g2, g3, g4 = grads(state, (1, 2, 3, 4), 4, 1, (h1, h2, h3, h4), (f32, f32, bf16, bf16))
    r3 = send(g3, BACK[3])
    r4 = send(g4, BACK[4])
    s1 = (g1 + jnp.where(turn, 0.0, r7.astype(f32)) + r5.astype(f32)).astype(bf16)
    s1, r7 = lax.optimization_barrier((s1, r7))
    r1 = send(s1, BACK[1])
    s2 = (g2 + jnp.where(turn, r7.astype(f32), 0.0) + r6.astype(f32)).astype(bf16)
    r2 = send(s2, BACK[2])
    rows[0], s2 = lax.optimization_barrier((rows[0], s2))
    (g0,) = grads(state, (0,), 4, 1, (h0,), (f32,))
    near = lax.optimization_barrier(g0 + r3.astype(f32) + r4.astype(f32))
    out = near + r1.astype(f32) + r2.astype(f32)
    return out.reshape(1, n, width)


def solution(mesh):
    in_specs = (P("con", "blk", None, None), P(), P(), P())

    return jax.shard_map(on_device, mesh=mesh, in_specs=in_specs, out_specs=P("con", "blk", None), check_vma=False)
```

```python
import functools
import jax
import jax.numpy as jnp
from jax import lax
from jax.experimental import pallas as pl
from jax.experimental.pallas import tpu as pltpu
from jax.sharding import PartitionSpec as P

AXES = ("blk", "con")
NX, NYH, NZ, NYL = 4, 2, 8, 2
VMEM_LIMIT = 14 * 1024 * 1024
NT = (((1,), (1,)), ((), ()))


def flat(x, yh, z, yl, c):
    return (((x % NX) * NYH + yh % NYH) * NZ + z % NZ) * 4 + yl * 2 + c


def send(v, ways):
    pairs = []
    for x in range(NX):
        for yh in range(NYH):
            for z in range(NZ):
                for yl in range(NYL):
                    for c, way in enumerate(ways):
                        dx, dy, dz = way(z) if callable(way) else way
                        pairs.append((flat(x, yh, z, yl, c), flat(x + dx, yh + dy, z + dz, yl, c)))
    return lax.ppermute(v, AXES, pairs)


def partner(v):
    return lax.ppermute(v, AXES, [(i, i ^ 1) for i in range(NX * NYH * NZ * 4)])


POOL_STEP = 48
PICK = 16


def pool_kernel(x_ref, o_ref, buf, sems):
    n, patches, width = buf.shape
    copies = [
        pltpu.make_async_copy(x_ref.at[pl.ds(i, POOL_STEP)], buf.at[pl.ds(i, POOL_STEP)], sems.at[i // POOL_STEP])
        for i in range(0, n, POOL_STEP)
    ]
    for copy in copies:
        copy.start()
    row = lax.broadcasted_iota(jnp.int32, (PICK, PICK * patches), 0) * patches
    col = lax.broadcasted_iota(jnp.int32, (PICK, PICK * patches), 1)
    pick = jnp.where((col >= row) & (col < row + patches), 1.0, 0.0).astype(jnp.bfloat16)
    for i in range(0, n, PICK):
        if i % POOL_STEP == 0:
            copies[i // POOL_STEP].wait()
        pooled = jnp.dot(pick, buf[i:i + PICK].reshape(PICK * patches, width), preferred_element_type=jnp.float32)
        pooled = pooled * (1.0 / patches)
        square = jnp.sum(pooled * pooled, axis=1, keepdims=True)
        o_ref[i:i + PICK, :] = (pooled * (1.0 / jnp.sqrt(square + 1e-06))).astype(o_ref.dtype)


def pool(rows):
    n, _, width = rows.shape
    return pl.pallas_call(
        pool_kernel,
        in_specs=[pl.BlockSpec(memory_space=pltpu.HBM)],
        out_specs=pl.BlockSpec(memory_space=pltpu.VMEM),
        out_shape=jax.ShapeDtypeStruct((n, width), jnp.bfloat16),
        scratch_shapes=[pltpu.VMEM(rows.shape, rows.dtype), pltpu.SemaphoreType.DMA((n // POOL_STEP,))],
        compiler_params=pltpu.CompilerParams(vmem_limit_bytes=60 * 1024 * 1024),
        cost_estimate=pl.CostEstimate(flops=2 * rows.size, bytes_accessed=2 * rows.size, transcendentals=0),
        name="pool",
    )(rows)


def grad_kernel(slots, first_col, groups, has_sum, par_ref, row_ref, col_ref, *refs):
    count = len(slots)
    s_refs, t_refs = refs[:count], refs[count:count + 4 * groups]
    sum_refs, o_refs = (refs[-2 * count:-count], refs[-count:]) if has_sum else (None, refs[-count:])
    pair = lax.axis_index("con") // 2
    scale, bias = par_ref[pl.ds(pair, 1), :], par_ref[pl.ds(pair + 2, 1), :]
    n = s_refs[0].shape[0]
    rows = jnp.concatenate([s[...] for s in s_refs], axis=0)
    row_ids = jnp.concatenate([row_ref[n * k:n * (k + 1), :] for k in slots], axis=0)
    total = jnp.concatenate([v[...] for v in sum_refs], axis=0) if has_sum else None
    for g in range(groups):
        cols = jnp.concatenate([t[...] for t in t_refs[4 * g:4 * g + 4]], axis=0)
        k = cols.shape[0]
        start = first_col * n + g * k
        dots = lax.dot_general(rows, cols, NT, preferred_element_type=jnp.float32)
        same = jnp.concatenate([row_ids] * (k // 128), axis=1) == col_ref[:, start:start + k]
        coeff = scale * jnp.tanh(scale * dots + bias) - jnp.where(same, scale, -scale)
        part = jnp.dot(coeff.astype(jnp.bfloat16), cols, preferred_element_type=jnp.float32)
        total = part if total is None else total + part
    for i, o_ref in enumerate(o_refs):
        o_ref[...] = total[n * i:n * (i + 1)].astype(o_ref.dtype)


def grads(state, slots, first_col, groups, sums, dtypes):
    par, row_ids, col_ids, rows, cols = state
    n, width = rows[0].shape
    count = len(slots)
    vmem = pl.BlockSpec(memory_space=pltpu.VMEM)
    operands = [rows[k] for k in slots] + cols[first_col:first_col + 4 * groups] + list(sums or [])
    return pl.pallas_call(
        functools.partial(grad_kernel, slots, first_col, groups, sums is not None),
        in_specs=[vmem] * (3 + len(operands)),
        out_specs=[vmem] * count,
        out_shape=[jax.ShapeDtypeStruct((n, width), dtype) for dtype in dtypes],
        compiler_params=pltpu.CompilerParams(vmem_limit_bytes=VMEM_LIMIT),
        cost_estimate=pl.CostEstimate(flops=16 * groups * count * n * n * width, bytes_accessed=4 * n * width * 2, transcendentals=4 * groups * count * n * n),
    )(par, row_ids, col_ids, *operands)


MOVES = {
    1: ((0, 0, 2), (0, 1, 0)), 2: ((0, 0, -2), (2, 0, 0)), 3: ((0, 0, 1), (1, 0, 0)), 4: ((0, 0, -1), (-1, 0, 0)),
    5: ((0, 0, 1), (1, 0, 0)), 6: ((0, 0, -1), (0, 1, 0)), 7: (lambda z: (0, 0, -2 if z % 2 else 2), (-1, 0, 0)),
}
BACK = {
    k: tuple(((lambda z, way=way: tuple(-d for d in way(z))) if callable(way) else tuple(-d for d in way)) for way in ways)
    for k, ways in MOVES.items()
}
Z_OFF = (0, -2, 2, -1, 1, -3, 3, -4)
X_OFF = (0, 0, 2, -1, 1, -1, 2, 1)
Y_OFF = (0, 1, 0, 0, 0, 1, 1, 1)


def on_device(patch_rows, subject_ids, logit_scale, logit_bias):
    n, _, width = patch_rows.shape[1:]
    f32, bf16 = jnp.float32, jnp.bfloat16
    own = pool(patch_rows[0])

    blk = lax.axis_index("blk")
    first = lax.axis_index("con") % 2 == 0
    x, yh, z = blk // 16, (blk // 8) % 2, blk % 8

    def ids(on_first):
        parts = []
        for zo, xo, yo in zip(Z_OFF, X_OFF, Y_OFF):
            on_z = (x * NYH + yh) * NZ + (z + zo) % NZ
            on_xy = (((x + xo) % NX) * NYH + (yh + yo) % NYH) * NZ + z
            parts.append(lax.dynamic_slice_in_dim(subject_ids, jnp.where(on_first, on_z, on_xy) * n, n, 0))
        return jnp.concatenate(parts)

    par = jnp.broadcast_to(jnp.concatenate([logit_scale, logit_bias])[:, None] * 0.5, (4, 4 * n))
    row_ids = jnp.broadcast_to(ids(first)[:, None], (8 * n, 128))
    col_ids = ids(jnp.logical_not(first))[None, :]

    rows = [own] + [None] * 7
    rows[1] = send(own, MOVES[1])
    rows[2] = send(own, MOVES[2])
    later, par, row_ids, col_ids = lax.optimization_barrier((own, par, row_ids, col_ids))
    rows[3] = send(later, MOVES[3])
    rows[4] = send(later, MOVES[4])
    rows[5] = send(rows[1], MOVES[5])
    turn = jnp.logical_and(first, z % 2 == 1)
    rows[7] = send(jnp.where(turn, rows[2], rows[1]), MOVES[7])
    rows[6] = send(rows[2], MOVES[6])
    cols = [partner(v) for v in rows[:5]]
    state = (par, row_ids, col_ids, rows, cols)
    near_slots, far_slots = (1, 2, 3, 4), (5, 6)
    h = grads(state, near_slots, 0, 1, None, (f32,) * 4)
    rows[5], rows[6], h = lax.optimization_barrier((rows[5], rows[6], h))
    cols += [partner(rows[k]) for k in far_slots]
    h5, h6 = grads(state, far_slots, 0, 1, None, (f32,) * 2)
    rows[7], h5, h6 = lax.optimization_barrier((rows[7], h5, h6))
    cols += [partner(rows[7])]
    (h7,) = grads(state, (7,), 0, 1, None, (f32,))
    g7, g5 = grads(state, (7, 5), 4, 1, (h7, h5), (bf16,) * 2)
    r7 = send(g7, BACK[7])
    rows[6], g5 = lax.optimization_barrier((rows[6], g5))
    r5 = send(g5, BACK[5])
    (g6,) = grads(state, (6,), 4, 1, (h6,), (bf16,))
    rows[1], g6 = lax.optimization_barrier((rows[1], g6))
    r6 = send(g6, BACK[6])
    g1, g2, g3, g4 = grads(state, near_slots, 4, 1, h, (f32, f32, bf16, bf16))
    rows[0], g1 = lax.optimization_barrier((rows[0], g1))
    (g0,) = grads(state, (0,), 0, 2, None, (f32,))
    g3, g4, g0 = lax.optimization_barrier((g3, g4, g0))
    r3 = send(g3, BACK[3])
    r4 = send(g4, BACK[4])
    s1 = (g1 + jnp.where(turn, 0.0, r7.astype(f32)) + r5.astype(f32)).astype(bf16)
    s1, r7 = lax.optimization_barrier((s1, r7))
    r1 = send(s1, BACK[1])
    s2 = (g2 + jnp.where(turn, r7.astype(f32), 0.0) + r6.astype(f32)).astype(bf16)
    r2 = send(s2, BACK[2])
    near = lax.optimization_barrier(g0 + r3.astype(f32) + r4.astype(f32))
    out = near + r1.astype(f32) + r2.astype(f32)
    return out.reshape(1, n, width)


def solution(mesh):
    in_specs = (P("con", "blk", None, None), P(), P(), P())

    return jax.shard_map(on_device, mesh=mesh, in_specs=in_specs, out_specs=P("con", "blk", None), check_vma=False)
```

```python
import functools
import jax
import jax.numpy as jnp
from jax import lax
from jax.experimental import pallas as pl
from jax.experimental.pallas import tpu as pltpu
from jax.sharding import PartitionSpec as P

AXES = ("blk", "con")
NX, NYH, NZ, NYL = 4, 2, 8, 2
VMEM_LIMIT = 14 * 1024 * 1024
NT = (((1,), (1,)), ((), ()))


def flat(x, yh, z, yl, c):
    return (((x % NX) * NYH + yh % NYH) * NZ + z % NZ) * 4 + yl * 2 + c


def send(v, ways, back=False):
    pairs = []
    for x in range(NX):
        for yh in range(NYH):
            for z in range(NZ):
                for yl in range(NYL):
                    for c, (dx, dy, dz) in enumerate((ways[0](z), ways[1])):
                        pair = flat(x, yh, z, yl, c), flat(x + dx, yh + dy, z + dz, yl, c)
                        pairs.append(pair[::-1] if back else pair)
    return lax.ppermute(v, AXES, pairs)


def partner(v):
    return lax.ppermute(v, AXES, [(i, i ^ 1) for i in range(NX * NYH * NZ * 4)])


POOL_STEP = 48
PICK = 16


def pool_kernel(x_ref, o_ref, buf, sems):
    n, patches, width = buf.shape
    copies = [
        pltpu.make_async_copy(x_ref.at[pl.ds(i, POOL_STEP)], buf.at[pl.ds(i, POOL_STEP)], sems.at[i // POOL_STEP])
        for i in range(0, n, POOL_STEP)
    ]
    for copy in copies:
        copy.start()
    row = lax.broadcasted_iota(jnp.int32, (PICK, PICK * patches), 0) * patches
    col = lax.broadcasted_iota(jnp.int32, (PICK, PICK * patches), 1)
    pick = jnp.where((col >= row) & (col < row + patches), 1.0, 0.0).astype(jnp.bfloat16)
    for i in range(0, n, PICK):
        if i % POOL_STEP == 0:
            copies[i // POOL_STEP].wait()
        pooled = jnp.dot(pick, buf[i:i + PICK].reshape(PICK * patches, width), preferred_element_type=jnp.float32)
        pooled = pooled * (1.0 / patches)
        square = jnp.sum(pooled * pooled, axis=1, keepdims=True)
        o_ref[i:i + PICK, :] = (pooled * (1.0 / jnp.sqrt(square + 1e-06))).astype(o_ref.dtype)


def pool(rows):
    n, _, width = rows.shape
    return pl.pallas_call(
        pool_kernel,
        in_specs=[pl.BlockSpec(memory_space=pltpu.HBM)],
        out_specs=pl.BlockSpec(memory_space=pltpu.VMEM),
        out_shape=jax.ShapeDtypeStruct((n, width), jnp.bfloat16),
        scratch_shapes=[pltpu.VMEM(rows.shape, rows.dtype), pltpu.SemaphoreType.DMA((n // POOL_STEP,))],
        compiler_params=pltpu.CompilerParams(vmem_limit_bytes=60 * 1024 * 1024),
        cost_estimate=pl.CostEstimate(flops=2 * rows.size, bytes_accessed=2 * rows.size, transcendentals=0),
        name="pool",
    )(rows)


def grad_kernel(slots, first_col, groups, has_sum, par_ref, row_ref, col_ref, *refs):
    count = len(slots)
    s_refs, t_refs = refs[:count], refs[count:count + 4 * groups]
    sum_refs, o_refs = (refs[-2 * count:-count], refs[-count:]) if has_sum else (None, refs[-count:])
    pair = lax.axis_index("con") // 2
    scale, bias = par_ref[pl.ds(pair, 1), :], par_ref[pl.ds(pair + 2, 1), :]
    n = s_refs[0].shape[0]
    rows = jnp.concatenate([s[...] for s in s_refs], axis=0)
    row_ids = jnp.concatenate([row_ref[n * k:n * (k + 1), :] for k in slots], axis=0)
    total = jnp.concatenate([v[...] for v in sum_refs], axis=0) if has_sum else None
    for g in range(groups):
        cols = jnp.concatenate([t[...] for t in t_refs[4 * g:4 * g + 4]], axis=0)
        k = cols.shape[0]
        start = first_col * n + g * k
        dots = lax.dot_general(rows, cols, NT, preferred_element_type=jnp.float32)
        same = jnp.concatenate([row_ids] * (k // 128), axis=1) == col_ref[:, start:start + k]
        coeff = scale * jnp.tanh(scale * dots + bias) - jnp.where(same, scale, -scale)
        part = jnp.dot(coeff.astype(jnp.bfloat16), cols, preferred_element_type=jnp.float32)
        total = part if total is None else total + part
    for i, o_ref in enumerate(o_refs):
        o_ref[...] = total[n * i:n * (i + 1)].astype(o_ref.dtype)


def grads(state, slots, first_col, groups, sums, dtypes):
    par, row_ids, col_ids, rows, cols = state
    n, width = rows[0].shape
    count = len(slots)
    vmem = pl.BlockSpec(memory_space=pltpu.VMEM)
    operands = [rows[k] for k in slots] + cols[first_col:first_col + 4 * groups] + list(sums or [])
    return pl.pallas_call(
        functools.partial(grad_kernel, slots, first_col, groups, sums is not None),
        in_specs=[vmem] * (3 + len(operands)),
        out_specs=[vmem] * count,
        out_shape=[jax.ShapeDtypeStruct((n, width), dtype) for dtype in dtypes],
        compiler_params=pltpu.CompilerParams(vmem_limit_bytes=VMEM_LIMIT),
        cost_estimate=pl.CostEstimate(flops=16 * groups * count * n * n * width, bytes_accessed=4 * n * width * 2, transcendentals=4 * groups * count * n * n),
    )(par, row_ids, col_ids, *operands)


def along_z(even, odd):
    return lambda z: (0, 0, odd if z % 2 else even)


MOVES = {
    1: (along_z(2, -2), (0, 1, 0)), 2: (along_z(-2, 2), (2, 0, 0)), 3: (along_z(1, 1), (1, 0, 0)), 4: (along_z(-1, -1), (-1, 0, 0)),
    5: (along_z(1, -1), (1, 0, 0)), 6: (along_z(-1, 1), (0, 1, 0)), 7: (along_z(2, -2), (-1, 0, 0)),
}
Z_EVEN = (0, -2, 2, -1, 1, 3, -3, 4)
Z_ODD = (0, 2, -2, -1, 1, -3, 3, 4)
X_OFF = (0, 0, 2, -1, 1, -1, 2, 1)
Y_OFF = (0, 1, 0, 0, 0, 1, 1, 1)


def on_device(patch_rows, subject_ids, logit_scale, logit_bias):
    n, _, width = patch_rows.shape[1:]
    f32, bf16 = jnp.float32, jnp.bfloat16
    own = pool(patch_rows[0])

    blk = lax.axis_index("blk")
    first = lax.axis_index("con") % 2 == 0
    x, yh, z = blk // 16, (blk // 8) % 2, blk % 8

    def ids(on_first):
        parts = []
        for even, odd, xo, yo in zip(Z_EVEN, Z_ODD, X_OFF, Y_OFF):
            on_z = (x * NYH + yh) * NZ + (z + jnp.where(z % 2 == 0, even, odd)) % NZ
            on_xy = (((x + xo) % NX) * NYH + (yh + yo) % NYH) * NZ + z
            parts.append(lax.dynamic_slice_in_dim(subject_ids, jnp.where(on_first, on_z, on_xy) * n, n, 0))
        return jnp.concatenate(parts)

    par = jnp.broadcast_to(jnp.concatenate([logit_scale, logit_bias])[:, None] * 0.5, (4, 4 * n))
    row_ids = jnp.broadcast_to(ids(first)[:, None], (8 * n, 128))
    col_ids = ids(jnp.logical_not(first))[None, :]

    rows = [own] + [None] * 7
    rows[1] = send(own, MOVES[1])
    rows[2] = send(own, MOVES[2])
    later, par, row_ids, col_ids = lax.optimization_barrier((own, par, row_ids, col_ids))
    rows[3] = send(later, MOVES[3])
    rows[4] = send(later, MOVES[4])
    rows[5] = send(rows[1], MOVES[5])
    rows[7] = send(rows[1], MOVES[7])
    rows[6] = send(rows[2], MOVES[6])
    cols = [partner(v) for v in rows[:5]]
    state = (par, row_ids, col_ids, rows, cols)
    h0, h3, h4 = grads(state, (0, 3, 4), 0, 1, None, (f32,) * 3)
    h1, h2 = grads(state, (1, 2), 0, 1, None, (f32,) * 2)
    rows[5], rows[6], rows[7], h0, h1, h2, h3, h4 = lax.optimization_barrier((rows[5], rows[6], rows[7], h0, h1, h2, h3, h4))
    cols += [partner(rows[k]) for k in (5, 6, 7)]
    h7, h5, h6 = grads(state, (7, 5, 6), 0, 1, None, (f32,) * 3)
    g7, g5, g6 = grads(state, (7, 5, 6), 4, 1, (h7, h5, h6), (bf16,) * 3)
    r7 = send(g7, MOVES[7], True)
    r5 = send(g5, MOVES[5], True)
    r6 = send(g6, MOVES[6], True)
    rows[1], g6 = lax.optimization_barrier((rows[1], g6))
    g1, g2, g3, g4 = grads(state, (1, 2, 3, 4), 4, 1, (h1, h2, h3, h4), (f32, f32, bf16, bf16))
    r3 = send(g3, MOVES[3], True)
    r4 = send(g4, MOVES[4], True)
    s1 = (g1 + r7.astype(f32) + r5.astype(f32)).astype(bf16)
    r1 = send(s1, MOVES[1], True)
    s2 = (g2 + r6.astype(f32)).astype(bf16)
    r2 = send(s2, MOVES[2], True)
    rows[0], s2 = lax.optimization_barrier((rows[0], s2))
    (g0,) = grads(state, (0,), 4, 1, (h0,), (f32,))
    near = lax.optimization_barrier(g0 + r3.astype(f32) + r4.astype(f32))
    out = near + r1.astype(f32) + r2.astype(f32)
    return out.reshape(1, n, width)


def solution(mesh):
    in_specs = (P("con", "blk", None, None), P(), P(), P())

    return jax.shard_map(on_device, mesh=mesh, in_specs=in_specs, out_specs=P("con", "blk", None), check_vma=False)
```

```python
import functools
import jax
import jax.numpy as jnp
from jax import lax
from jax.experimental import pallas as pl
from jax.experimental.pallas import tpu as pltpu
from jax.sharding import PartitionSpec as P

AXES = ("blk", "con")
NX, NYH, NZ, NYL = 4, 2, 8, 2
VMEM_LIMIT = 14 * 1024 * 1024
NT = (((1,), (1,)), ((), ()))


def flat(x, yh, z, yl, c):
    return (((x % NX) * NYH + yh % NYH) * NZ + z % NZ) * 4 + yl * 2 + c


def send(v, ways, back=False):
    pairs = []
    for x in range(NX):
        for yh in range(NYH):
            for z in range(NZ):
                for yl in range(NYL):
                    for c, (dx, dy, dz) in enumerate((ways[0](z), ways[1])):
                        pair = flat(x, yh, z, yl, c), flat(x + dx, yh + dy, z + dz, yl, c)
                        pairs.append(pair[::-1] if back else pair)
    return lax.ppermute(v, AXES, pairs)


def partner(v):
    return lax.ppermute(v, AXES, [(i, i ^ 1) for i in range(NX * NYH * NZ * 4)])


POOL_STEP = 48
PICK = 16


def pool_kernel(x_ref, o_ref, buf, sems):
    n, patches, width = buf.shape
    copies = [
        pltpu.make_async_copy(x_ref.at[pl.ds(i, POOL_STEP)], buf.at[pl.ds(i, POOL_STEP)], sems.at[i // POOL_STEP])
        for i in range(0, n, POOL_STEP)
    ]
    for copy in copies:
        copy.start()
    row = lax.broadcasted_iota(jnp.int32, (PICK, PICK * patches), 0) * patches
    col = lax.broadcasted_iota(jnp.int32, (PICK, PICK * patches), 1)
    pick = jnp.where((col >= row) & (col < row + patches), 1.0, 0.0).astype(jnp.bfloat16)
    for i in range(0, n, PICK):
        if i % POOL_STEP == 0:
            copies[i // POOL_STEP].wait()
        pooled = jnp.dot(pick, buf[i:i + PICK].reshape(PICK * patches, width), preferred_element_type=jnp.float32)
        pooled = pooled * (1.0 / patches)
        square = jnp.sum(pooled * pooled, axis=1, keepdims=True)
        o_ref[i:i + PICK, :] = (pooled * (1.0 / jnp.sqrt(square + 1e-06))).astype(o_ref.dtype)


def pool(rows):
    n, _, width = rows.shape
    return pl.pallas_call(
        pool_kernel,
        in_specs=[pl.BlockSpec(memory_space=pltpu.HBM)],
        out_specs=pl.BlockSpec(memory_space=pltpu.VMEM),
        out_shape=jax.ShapeDtypeStruct((n, width), jnp.bfloat16),
        scratch_shapes=[pltpu.VMEM(rows.shape, rows.dtype), pltpu.SemaphoreType.DMA((n // POOL_STEP,))],
        compiler_params=pltpu.CompilerParams(vmem_limit_bytes=60 * 1024 * 1024),
        cost_estimate=pl.CostEstimate(flops=2 * rows.size, bytes_accessed=2 * rows.size, transcendentals=0),
        name="pool",
    )(rows)


def grad_kernel(slots, first_col, groups, has_sum, par_ref, row_ref, col_ref, *refs):
    count = len(slots)
    s_refs, t_refs = refs[:count], refs[count:count + 4 * groups]
    sum_refs, o_refs = (refs[-2 * count:-count], refs[-count:]) if has_sum else (None, refs[-count:])
    pair = lax.axis_index("con") // 2
    scale, bias = par_ref[pl.ds(pair, 1), :], par_ref[pl.ds(pair + 2, 1), :]
    n = s_refs[0].shape[0]
    rows = jnp.concatenate([s[...] for s in s_refs], axis=0)
    row_ids = jnp.concatenate([row_ref[n * k:n * (k + 1), :] for k in slots], axis=0)
    total = jnp.concatenate([v[...] for v in sum_refs], axis=0) if has_sum else None
    for g in range(groups):
        cols = jnp.concatenate([t[...] for t in t_refs[4 * g:4 * g + 4]], axis=0)
        k = cols.shape[0]
        start = first_col * n + g * k
        dots = lax.dot_general(rows, cols, NT, preferred_element_type=jnp.float32)
        same = jnp.concatenate([row_ids] * (k // 128), axis=1) == col_ref[:, start:start + k]
        coeff = scale * jnp.tanh(scale * dots + bias) - jnp.where(same, scale, -scale)
        part = jnp.dot(coeff.astype(jnp.bfloat16), cols, preferred_element_type=jnp.float32)
        total = part if total is None else total + part
    for i, o_ref in enumerate(o_refs):
        o_ref[...] = total[n * i:n * (i + 1)].astype(o_ref.dtype)


def grads(state, slots, first_col, groups, sums, dtypes):
    par, row_ids, col_ids, rows, cols = state
    n, width = rows[0].shape
    count = len(slots)
    vmem = pl.BlockSpec(memory_space=pltpu.VMEM)
    operands = [rows[k] for k in slots] + cols[first_col:first_col + 4 * groups] + list(sums or [])
    return pl.pallas_call(
        functools.partial(grad_kernel, slots, first_col, groups, sums is not None),
        in_specs=[vmem] * (3 + len(operands)),
        out_specs=[vmem] * count,
        out_shape=[jax.ShapeDtypeStruct((n, width), dtype) for dtype in dtypes],
        compiler_params=pltpu.CompilerParams(vmem_limit_bytes=VMEM_LIMIT),
        cost_estimate=pl.CostEstimate(flops=16 * groups * count * n * n * width, bytes_accessed=4 * n * width * 2, transcendentals=4 * groups * count * n * n),
    )(par, row_ids, col_ids, *operands)


def along_z(even, odd):
    return lambda z: (0, 0, odd if z % 2 else even)


MOVES = {
    1: (along_z(2, -2), (0, 1, 0)), 2: (along_z(-2, 2), (2, 0, 0)), 3: (along_z(1, 1), (1, 0, 0)), 4: (along_z(-1, -1), (-1, 0, 0)),
    5: (along_z(1, -1), (1, 0, 0)), 6: (along_z(-1, 1), (0, 1, 0)), 7: (along_z(2, -2), (-1, 0, 0)),
}
Z_EVEN = (0, -2, 2, -1, 1, 3, -3, 4)
Z_ODD = (0, 2, -2, -1, 1, -3, 3, 4)
X_OFF = (0, 0, 2, -1, 1, -1, 2, 1)
Y_OFF = (0, 1, 0, 0, 0, 1, 1, 1)


def on_device(patch_rows, subject_ids, logit_scale, logit_bias):
    n, _, width = patch_rows.shape[1:]
    f32, bf16 = jnp.float32, jnp.bfloat16
    own = pool(patch_rows[0])

    blk = lax.axis_index("blk")
    first = lax.axis_index("con") % 2 == 0
    x, yh, z = blk // 16, (blk // 8) % 2, blk % 8

    def ids(on_first):
        parts = []
        for even, odd, xo, yo in zip(Z_EVEN, Z_ODD, X_OFF, Y_OFF):
            on_z = (x * NYH + yh) * NZ + (z + jnp.where(z % 2 == 0, even, odd)) % NZ
            on_xy = (((x + xo) % NX) * NYH + (yh + yo) % NYH) * NZ + z
            parts.append(lax.dynamic_slice_in_dim(subject_ids, jnp.where(on_first, on_z, on_xy) * n, n, 0))
        return jnp.concatenate(parts)

    par = jnp.broadcast_to(jnp.concatenate([logit_scale, logit_bias])[:, None] * 0.5, (4, 4 * n))
    row_ids = jnp.broadcast_to(ids(first)[:, None], (8 * n, 128))
    col_ids = ids(jnp.logical_not(first))[None, :]

    rows = [own] + [None] * 7
    rows[1] = send(own, MOVES[1])
    later, par, row_ids, col_ids = lax.optimization_barrier((own, par, row_ids, col_ids))
    rows[2] = send(later, MOVES[2])
    rows[3] = send(later, MOVES[3])
    rows[4] = send(later, MOVES[4])
    rows[5] = send(rows[1], MOVES[5])
    rows[7] = send(rows[1], MOVES[7])
    rows[6] = send(rows[2], MOVES[6])
    cols = [partner(v) for v in rows[:5]]
    state = (par, row_ids, col_ids, rows, cols)
    h0, h3, h4 = grads(state, (0, 3, 4), 0, 1, None, (f32,) * 3)
    h1, h2 = grads(state, (1, 2), 0, 1, None, (f32,) * 2)
    rows[5], rows[6], rows[7], h0, h1, h2, h3, h4 = lax.optimization_barrier((rows[5], rows[6], rows[7], h0, h1, h2, h3, h4))
    cols += [partner(rows[k]) for k in (5, 6, 7)]
    h7, h5, h6 = grads(state, (7, 5, 6), 0, 1, None, (f32,) * 3)
    (g7,) = grads(state, (7,), 4, 1, (h7,), (bf16,))
    rows[5], g7 = lax.optimization_barrier((rows[5], g7))
    r7 = send(g7, MOVES[7], True)
    g5, g6 = grads(state, (5, 6), 4, 1, (h5, h6), (bf16,) * 2)
    rows[3], g5, g6 = lax.optimization_barrier((rows[3], g5, g6))
    r5 = send(g5, MOVES[5], True)
    r6 = send(g6, MOVES[6], True)
    g3, g4 = grads(state, (3, 4), 4, 1, (h3, h4), (bf16,) * 2)
    rows[1], g3, g4 = lax.optimization_barrier((rows[1], g3, g4))
    r3 = send(g3, MOVES[3], True)
    r4 = send(g4, MOVES[4], True)
    g1, g2 = grads(state, (1, 2), 4, 1, (h1, h2), (f32,) * 2)
    s1 = (g1 + r7.astype(f32) + r5.astype(f32)).astype(bf16)
    r1 = send(s1, MOVES[1], True)
    s2 = (g2 + r6.astype(f32)).astype(bf16)
    r2 = send(s2, MOVES[2], True)
    rows[0], s2 = lax.optimization_barrier((rows[0], s2))
    (g0,) = grads(state, (0,), 4, 1, (h0,), (f32,))
    near = lax.optimization_barrier(g0 + r3.astype(f32) + r4.astype(f32))
    out = near + r1.astype(f32) + r2.astype(f32)
    return out.reshape(1, n, width)


def solution(mesh):
    in_specs = (P("con", "blk", None, None), P(), P(), P())

    return jax.shard_map(on_device, mesh=mesh, in_specs=in_specs, out_specs=P("con", "blk", None), check_vma=False)
```

```python
import functools
import jax
import jax.numpy as jnp
from jax import lax
from jax.experimental import pallas as pl
from jax.experimental.pallas import tpu as pltpu
from jax.sharding import PartitionSpec as P

AXES = ("blk", "con")
NX, NYH, NZ, NYL = 4, 2, 8, 2
VMEM_LIMIT = 14 * 1024 * 1024
NT = (((1,), (1,)), ((), ()))


def flat(x, yh, z, yl, c):
    return (((x % NX) * NYH + yh % NYH) * NZ + z % NZ) * 4 + yl * 2 + c


def send(v, ways, back=False):
    pairs = []
    for x in range(NX):
        for yh in range(NYH):
            for z in range(NZ):
                for yl in range(NYL):
                    for c, (dx, dy, dz) in enumerate((ways[0](z), ways[1])):
                        pair = flat(x, yh, z, yl, c), flat(x + dx, yh + dy, z + dz, yl, c)
                        pairs.append(pair[::-1] if back else pair)
    return lax.ppermute(v, AXES, pairs)


def partner(v):
    return lax.ppermute(v, AXES, [(i, i ^ 1) for i in range(NX * NYH * NZ * 4)])


POOL_STEP = 48
PICK = 16


def pool_kernel(x_ref, o_ref, buf, sems):
    n, patches, width = buf.shape
    copies = [
        pltpu.make_async_copy(x_ref.at[pl.ds(i, POOL_STEP)], buf.at[pl.ds(i, POOL_STEP)], sems.at[i // POOL_STEP])
        for i in range(0, n, POOL_STEP)
    ]
    for copy in copies:
        copy.start()
    row = lax.broadcasted_iota(jnp.int32, (PICK, PICK * patches), 0) * patches
    col = lax.broadcasted_iota(jnp.int32, (PICK, PICK * patches), 1)
    pick = jnp.where((col >= row) & (col < row + patches), 1.0, 0.0).astype(jnp.bfloat16)
    for i in range(0, n, PICK):
        if i % POOL_STEP == 0:
            copies[i // POOL_STEP].wait()
        pooled = jnp.dot(pick, buf[i:i + PICK].reshape(PICK * patches, width), preferred_element_type=jnp.float32)
        pooled = pooled * (1.0 / patches)
        square = jnp.sum(pooled * pooled, axis=1, keepdims=True)
        o_ref[i:i + PICK, :] = (pooled * (1.0 / jnp.sqrt(square + 1e-06))).astype(o_ref.dtype)


def pool(rows):
    n, _, width = rows.shape
    return pl.pallas_call(
        pool_kernel,
        in_specs=[pl.BlockSpec(memory_space=pltpu.HBM)],
        out_specs=pl.BlockSpec(memory_space=pltpu.VMEM),
        out_shape=jax.ShapeDtypeStruct((n, width), jnp.bfloat16),
        scratch_shapes=[pltpu.VMEM(rows.shape, rows.dtype), pltpu.SemaphoreType.DMA((n // POOL_STEP,))],
        compiler_params=pltpu.CompilerParams(vmem_limit_bytes=60 * 1024 * 1024),
        cost_estimate=pl.CostEstimate(flops=2 * rows.size, bytes_accessed=2 * rows.size, transcendentals=0),
        name="pool",
    )(rows)


def grad_kernel(slots, first_col, groups, has_sum, par_ref, row_ref, col_ref, *refs):
    count = len(slots)
    s_refs, t_refs = refs[:count], refs[count:count + 4 * groups]
    sum_refs, o_refs = (refs[-2 * count:-count], refs[-count:]) if has_sum else (None, refs[-count:])
    pair = lax.axis_index("con") // 2
    scale, bias = par_ref[pl.ds(pair, 1), :], par_ref[pl.ds(pair + 2, 1), :]
    n = s_refs[0].shape[0]
    rows = jnp.concatenate([s[...] for s in s_refs], axis=0)
    row_ids = jnp.concatenate([row_ref[n * k:n * (k + 1), :] for k in slots], axis=0)
    total = jnp.concatenate([v[...] for v in sum_refs], axis=0) if has_sum else None
    for g in range(groups):
        cols = jnp.concatenate([t[...] for t in t_refs[4 * g:4 * g + 4]], axis=0)
        k = cols.shape[0]
        start = first_col * n + g * k
        dots = lax.dot_general(rows, cols, NT, preferred_element_type=jnp.float32)
        same = jnp.concatenate([row_ids] * (k // 128), axis=1) == col_ref[:, start:start + k]
        coeff = scale * jnp.tanh(scale * dots + bias) - jnp.where(same, scale, -scale)
        part = jnp.dot(coeff.astype(jnp.bfloat16), cols, preferred_element_type=jnp.float32)
        total = part if total is None else total + part
    for i, o_ref in enumerate(o_refs):
        o_ref[...] = total[n * i:n * (i + 1)].astype(o_ref.dtype)


def grads(state, slots, first_col, groups, sums, dtypes):
    par, row_ids, col_ids, rows, cols = state
    n, width = rows[0].shape
    count = len(slots)
    vmem = pl.BlockSpec(memory_space=pltpu.VMEM)
    operands = [rows[k] for k in slots] + cols[first_col:first_col + 4 * groups] + list(sums or [])
    return pl.pallas_call(
        functools.partial(grad_kernel, slots, first_col, groups, sums is not None),
        in_specs=[vmem] * (3 + len(operands)),
        out_specs=[vmem] * count,
        out_shape=[jax.ShapeDtypeStruct((n, width), dtype) for dtype in dtypes],
        compiler_params=pltpu.CompilerParams(vmem_limit_bytes=VMEM_LIMIT),
        cost_estimate=pl.CostEstimate(flops=16 * groups * count * n * n * width, bytes_accessed=4 * n * width * 2, transcendentals=4 * groups * count * n * n),
    )(par, row_ids, col_ids, *operands)


def along_z(even, odd):
    return lambda z: (0, 0, odd if z % 2 else even)


MOVES = {
    1: (along_z(2, -2), (0, 1, 0)), 2: (along_z(-2, 2), (2, 0, 0)), 3: (along_z(1, 1), (1, 0, 0)), 4: (along_z(-1, -1), (-1, 0, 0)),
    5: (along_z(1, -1), (1, 0, 0)), 6: (along_z(-1, 1), (0, 1, 0)), 7: (along_z(2, -2), (-1, 0, 0)),
}
Z_EVEN = (0, -2, 2, -1, 1, 3, -3, 4)
Z_ODD = (0, 2, -2, -1, 1, -3, 3, 4)
X_OFF = (0, 0, 2, -1, 1, -1, 2, 1)
Y_OFF = (0, 1, 0, 0, 0, 1, 1, 1)


COLS = (0, 1, 2, 5, 7, 6, 3, 4)


def on_device(patch_rows, subject_ids, logit_scale, logit_bias):
    n, _, width = patch_rows.shape[1:]
    f32, bf16 = jnp.float32, jnp.bfloat16
    own = pool(patch_rows[0])

    blk = lax.axis_index("blk")
    first = lax.axis_index("con") % 2 == 0
    x, yh, z = blk // 16, (blk // 8) % 2, blk % 8

    def ids(on_first, slots):
        parts = []
        for even, odd, xo, yo in [(Z_EVEN[k], Z_ODD[k], X_OFF[k], Y_OFF[k]) for k in slots]:
            on_z = (x * NYH + yh) * NZ + (z + jnp.where(z % 2 == 0, even, odd)) % NZ
            on_xy = (((x + xo) % NX) * NYH + (yh + yo) % NYH) * NZ + z
            parts.append(lax.dynamic_slice_in_dim(subject_ids, jnp.where(on_first, on_z, on_xy) * n, n, 0))
        return jnp.concatenate(parts)

    par = jnp.broadcast_to(jnp.concatenate([logit_scale, logit_bias])[:, None] * 0.5, (4, 4 * n))
    row_ids = jnp.broadcast_to(ids(first, range(8))[:, None], (8 * n, 128))
    col_ids = ids(jnp.logical_not(first), COLS)[None, :]

    rows = [own] + [None] * 7
    rows[1] = send(own, MOVES[1])
    later, par, row_ids, col_ids = lax.optimization_barrier((own, par, row_ids, col_ids))
    rows[2] = send(later, MOVES[2])
    rows[3] = send(later, MOVES[3])
    rows[4] = send(later, MOVES[4])
    rows[5] = send(rows[1], MOVES[5])
    rows[7] = send(rows[1], MOVES[7])
    rows[6] = send(rows[2], MOVES[6])
    cols = [partner(rows[k]) for k in (0, 1, 2, 5)]
    state = (par, row_ids, col_ids, rows, cols)
    h0, h1, h2 = grads(state, (0, 1, 2), 0, 1, None, (f32,) * 3)
    rows[7], rows[6], h0, h1, h2 = lax.optimization_barrier((rows[7], rows[6], h0, h1, h2))
    cols += [partner(rows[k]) for k in (7, 6)]
    h7, h5, h6 = grads(state, (7, 5, 6), 0, 1, None, (f32,) * 3)
    rows[3], rows[4], h7, h5, h6 = lax.optimization_barrier((rows[3], rows[4], h7, h5, h6))
    cols += [partner(rows[k]) for k in (3, 4)]
    h3, h4 = grads(state, (3, 4), 0, 1, None, (f32,) * 2)
    h7, h3, h4 = lax.optimization_barrier((h7, h3, h4))
    (g7,) = grads(state, (7,), 4, 1, (h7,), (bf16,))
    rows[5], g7 = lax.optimization_barrier((rows[5], g7))
    r7 = send(g7, MOVES[7], True)
    g5, g6 = grads(state, (5, 6), 4, 1, (h5, h6), (bf16,) * 2)
    rows[3], g5, g6 = lax.optimization_barrier((rows[3], g5, g6))
    r5 = send(g5, MOVES[5], True)
    r6 = send(g6, MOVES[6], True)
    g3, g4 = grads(state, (3, 4), 4, 1, (h3, h4), (bf16,) * 2)
    rows[1], g3, g4 = lax.optimization_barrier((rows[1], g3, g4))
    r3 = send(g3, MOVES[3], True)
    r4 = send(g4, MOVES[4], True)
    g1, g2 = grads(state, (1, 2), 4, 1, (h1, h2), (f32,) * 2)
    s1 = (g1 + r7.astype(f32) + r5.astype(f32)).astype(bf16)
    r1 = send(s1, MOVES[1], True)
    s2 = (g2 + r6.astype(f32)).astype(bf16)
    r2 = send(s2, MOVES[2], True)
    rows[0], s2 = lax.optimization_barrier((rows[0], s2))
    (g0,) = grads(state, (0,), 4, 1, (h0,), (f32,))
    near = lax.optimization_barrier(g0 + r3.astype(f32) + r4.astype(f32))
    out = near + r1.astype(f32) + r2.astype(f32)
    return out.reshape(1, n, width)


def solution(mesh):
    in_specs = (P("con", "blk", None, None), P(), P(), P())

    return jax.shard_map(on_device, mesh=mesh, in_specs=in_specs, out_specs=P("con", "blk", None), check_vma=False)
```

```python
import functools
import jax
import jax.numpy as jnp
from jax import lax
from jax.experimental import pallas as pl
from jax.experimental.pallas import tpu as pltpu
from jax.sharding import PartitionSpec as P

AXES = ("blk", "con")
NX, NYH, NZ, NYL = 4, 2, 8, 2
VMEM_LIMIT = 14 * 1024 * 1024
NT = (((1,), (1,)), ((), ()))


def flat(x, yh, z, yl, c):
    return (((x % NX) * NYH + yh % NYH) * NZ + z % NZ) * 4 + yl * 2 + c


def send(v, ways):
    pairs = []
    for x in range(NX):
        for yh in range(NYH):
            for z in range(NZ):
                for yl in range(NYL):
                    for c, way in enumerate(ways):
                        dx, dy, dz = way(z) if callable(way) else way
                        pairs.append((flat(x, yh, z, yl, c), flat(x + dx, yh + dy, z + dz, yl, c)))
    return lax.ppermute(v, AXES, pairs)


def partner(v):
    return lax.ppermute(v, AXES, [(i, i ^ 1) for i in range(NX * NYH * NZ * 4)])


POOL_STEP = 48
PICK = 16


def pool_kernel(x_ref, o_ref, buf, sems):
    n, patches, width = buf.shape
    copies = [
        pltpu.make_async_copy(x_ref.at[pl.ds(i, POOL_STEP)], buf.at[pl.ds(i, POOL_STEP)], sems.at[i // POOL_STEP])
        for i in range(0, n, POOL_STEP)
    ]
    for copy in copies:
        copy.start()
    row = lax.broadcasted_iota(jnp.int32, (PICK, PICK * patches), 0) * patches
    col = lax.broadcasted_iota(jnp.int32, (PICK, PICK * patches), 1)
    pick = jnp.where((col >= row) & (col < row + patches), 1.0, 0.0).astype(jnp.bfloat16)
    for i in range(0, n, PICK):
        if i % POOL_STEP == 0:
            copies[i // POOL_STEP].wait()
        pooled = jnp.dot(pick, buf[i:i + PICK].reshape(PICK * patches, width), preferred_element_type=jnp.float32)
        pooled = pooled * (1.0 / patches)
        square = jnp.sum(pooled * pooled, axis=1, keepdims=True)
        o_ref[i:i + PICK, :] = (pooled * (1.0 / jnp.sqrt(square + 1e-06))).astype(o_ref.dtype)


def pool(rows):
    n, _, width = rows.shape
    return pl.pallas_call(
        pool_kernel,
        in_specs=[pl.BlockSpec(memory_space=pltpu.HBM)],
        out_specs=pl.BlockSpec(memory_space=pltpu.VMEM),
        out_shape=jax.ShapeDtypeStruct((n, width), jnp.bfloat16),
        scratch_shapes=[pltpu.VMEM(rows.shape, rows.dtype), pltpu.SemaphoreType.DMA((n // POOL_STEP,))],
        compiler_params=pltpu.CompilerParams(vmem_limit_bytes=60 * 1024 * 1024),
        cost_estimate=pl.CostEstimate(flops=2 * rows.size, bytes_accessed=2 * rows.size, transcendentals=0),
        name="pool",
    )(rows)


def grad_kernel(slots, first_col, groups, has_sum, par_ref, row_ref, col_ref, *refs):
    count = len(slots)
    s_refs, t_refs = refs[:count], refs[count:count + 4 * groups]
    sum_refs, o_refs = (refs[-2 * count:-count], refs[-count:]) if has_sum else (None, refs[-count:])
    pair = lax.axis_index("con") // 2
    scale, bias = par_ref[pl.ds(pair, 1), :], par_ref[pl.ds(pair + 2, 1), :]
    n = s_refs[0].shape[0]
    rows = jnp.concatenate([s[...] for s in s_refs], axis=0)
    row_ids = jnp.concatenate([row_ref[n * k:n * (k + 1), :] for k in slots], axis=0)
    total = jnp.concatenate([v[...] for v in sum_refs], axis=0) if has_sum else None
    for g in range(groups):
        cols = jnp.concatenate([t[...] for t in t_refs[4 * g:4 * g + 4]], axis=0)
        k = cols.shape[0]
        start = first_col * n + g * k
        dots = lax.dot_general(rows, cols, NT, preferred_element_type=jnp.float32)
        same = jnp.concatenate([row_ids] * (k // 128), axis=1) == col_ref[:, start:start + k]
        coeff = scale * jnp.tanh(scale * dots + bias) - jnp.where(same, scale, -scale)
        part = jnp.dot(coeff.astype(jnp.bfloat16), cols, preferred_element_type=jnp.float32)
        total = part if total is None else total + part
    for i, o_ref in enumerate(o_refs):
        o_ref[...] = total[n * i:n * (i + 1)].astype(o_ref.dtype)


def grads(state, slots, first_col, groups, sums, dtypes):
    par, row_ids, col_ids, rows, cols = state
    n, width = rows[0].shape
    count = len(slots)
    vmem = pl.BlockSpec(memory_space=pltpu.VMEM)
    operands = [rows[k] for k in slots] + cols[first_col:first_col + 4 * groups] + list(sums or [])
    return pl.pallas_call(
        functools.partial(grad_kernel, slots, first_col, groups, sums is not None),
        in_specs=[vmem] * (3 + len(operands)),
        out_specs=[vmem] * count,
        out_shape=[jax.ShapeDtypeStruct((n, width), dtype) for dtype in dtypes],
        compiler_params=pltpu.CompilerParams(vmem_limit_bytes=VMEM_LIMIT),
        cost_estimate=pl.CostEstimate(flops=16 * groups * count * n * n * width, bytes_accessed=4 * n * width * 2, transcendentals=4 * groups * count * n * n),
    )(par, row_ids, col_ids, *operands)


MOVES = {
    1: ((0, 0, 2), (0, 1, 0)), 2: ((0, 0, -2), (2, 0, 0)), 3: ((0, 0, 1), (1, 0, 0)), 4: ((0, 0, -1), (-1, 0, 0)),
    5: ((0, 0, 1), (1, 0, 0)), 6: ((0, 0, -1), (0, 1, 0)), 7: (lambda z: (0, 0, -2 if z % 2 else 2), (-1, 0, 0)),
}
BACK = {
    k: tuple(((lambda z, way=way: tuple(-d for d in way(z))) if callable(way) else tuple(-d for d in way)) for way in ways)
    for k, ways in MOVES.items()
}
Z_OFF = (0, -2, 2, -1, 1, -3, 3, -4)
X_OFF = (0, 0, 2, -1, 1, -1, 2, 1)
Y_OFF = (0, 1, 0, 0, 0, 1, 1, 1)


def on_device(patch_rows, subject_ids, logit_scale, logit_bias):
    n, _, width = patch_rows.shape[1:]
    f32, bf16 = jnp.float32, jnp.bfloat16
    own = pool(patch_rows[0])

    blk = lax.axis_index("blk")
    first = lax.axis_index("con") % 2 == 0
    x, yh, z = blk // 16, (blk // 8) % 2, blk % 8

    def ids(on_first):
        parts = []
        for zo, xo, yo in zip(Z_OFF, X_OFF, Y_OFF):
            on_z = (x * NYH + yh) * NZ + (z + zo) % NZ
            on_xy = (((x + xo) % NX) * NYH + (yh + yo) % NYH) * NZ + z
            parts.append(lax.dynamic_slice_in_dim(subject_ids, jnp.where(on_first, on_z, on_xy) * n, n, 0))
        return jnp.concatenate(parts)

    par = jnp.broadcast_to(jnp.concatenate([logit_scale, logit_bias])[:, None] * 0.5, (4, 4 * n))
    row_ids = jnp.broadcast_to(ids(first)[:, None], (8 * n, 128))
    col_ids = ids(jnp.logical_not(first))[None, :]

    rows = [own] + [None] * 7
    rows[1] = send(own, MOVES[1])
    rows[2] = send(own, MOVES[2])
    later, par, row_ids, col_ids = lax.optimization_barrier((own, par, row_ids, col_ids))
    rows[3] = send(later, MOVES[3])
    rows[4] = send(later, MOVES[4])
    rows[5] = send(rows[1], MOVES[5])
    turn = jnp.logical_and(first, z % 2 == 1)
    rows[7] = send(jnp.where(turn, rows[2], rows[1]), MOVES[7])
    rows[6] = send(rows[2], MOVES[6])
    cols = [partner(v) for v in rows[:5]]
    state = (par, row_ids, col_ids, rows, cols)
    h0, h3, h4 = grads(state, (0, 3, 4), 0, 1, None, (f32,) * 3)
    h1, h2 = grads(state, (1, 2), 0, 1, None, (f32,) * 2)
    rows[5], rows[6], rows[7], h0, h1, h2, h3, h4 = lax.optimization_barrier((rows[5], rows[6], rows[7], h0, h1, h2, h3, h4))
    cols += [partner(rows[k]) for k in (5, 6, 7)]
    h7, h5, h6 = grads(state, (7, 5, 6), 0, 1, None, (f32,) * 3)
    (g7,) = grads(state, (7,), 4, 1, (h7,), (bf16,))
    rows[5], g7 = lax.optimization_barrier((rows[5], g7))
    r7 = send(g7, BACK[7])
    g5, g6 = grads(state, (5, 6), 4, 1, (h5, h6), (bf16,) * 2)
    rows[3], g5, g6 = lax.optimization_barrier((rows[3], g5, g6))
    r5 = send(g5, BACK[5])
    r6 = send(g6, BACK[6])
    g3, g4 = grads(state, (3, 4), 4, 1, (h3, h4), (bf16,) * 2)
    rows[1], g3, g4 = lax.optimization_barrier((rows[1], g3, g4))
    r3 = send(g3, BACK[3])
    r4 = send(g4, BACK[4])
    g1, g2 = grads(state, (1, 2), 4, 1, (h1, h2), (f32,) * 2)
    s1 = (g1 + jnp.where(turn, 0.0, r7.astype(f32)) + r5.astype(f32)).astype(bf16)
    s1, r7 = lax.optimization_barrier((s1, r7))
    r1 = send(s1, BACK[1])
    s2 = (g2 + jnp.where(turn, r7.astype(f32), 0.0) + r6.astype(f32)).astype(bf16)
    r2 = send(s2, BACK[2])
    rows[0], s2 = lax.optimization_barrier((rows[0], s2))
    (g0,) = grads(state, (0,), 4, 1, (h0,), (f32,))
    near = lax.optimization_barrier(g0 + r3.astype(f32) + r4.astype(f32))
    out = near + r1.astype(f32) + r2.astype(f32)
    return out.reshape(1, n, width)


def solution(mesh):
    in_specs = (P("con", "blk", None, None), P(), P(), P())

    return jax.shard_map(on_device, mesh=mesh, in_specs=in_specs, out_specs=P("con", "blk", None), check_vma=False)
```
